32 devices in a mesh: segment: 8 (over z, y), band: 4 (over x, core).
Axes of the slice: x: 2, y: 2, z: 4, core: 2. Of those that a mesh axis runs over, the one named last changes fastest.
Arguments:
- forward_state: bfloat16 [8, 2, 32, 64, 256], P('segment', None, 'band'), may hold values from -6 to 6
- returning_state: bfloat16 [8, 2, 32, 64, 256], P('segment', None, 'band'), may hold values from -6 to 6
- returning_grad: bfloat16 [8, 2, 32, 64, 256], P('segment', None, 'band'), may hold values from -6 to 6
- weights: bfloat16 [8, 2, 2304, 256], P('segment'), may hold values from -0.125 to 0.125
- fresh_input: bfloat16 [2, 2, 32, 64, 256], P(None, None, 'band'), may hold values from -6 to 6
- loss_grad: bfloat16 [2, 2, 32, 64, 256], P(None, None, 'band'), may hold values from -6 to 6
Outputs:
- forward_out: bfloat16 [8, 2, 32, 64, 256], P('segment', None, 'band')
- returning_out: bfloat16 [8, 2, 32, 64, 256], P('segment', None, 'band')
- backward_out: bfloat16 [8, 2, 32, 64, 256], P('segment', None, 'band')
- weight_grad: float32 [8, 2, 2304, 256], P('segment', None, 'band')
The draws below stay inside these ranges and needn't reach their ends.
All inputs are finite; a program needn't handle non-finite values.
Results may differ from the reference program's by a relative error of at most 0.02.
Values may be sent and summed in bfloat16 or wider, within the bound.
A program may use at most 64 MiB of HBM per device.

```python
import jax
import jax.numpy as jnp
from jax import lax

CHANNELS = 256
TILE_COLS = 64
TICK_COUNT = 2
SEGMENTS = 8
HEIGHT = 32


def shard_levels(rng, shape, split, low, largest):
    def one(axis_at, shards_of):
        heights = jax.random.uniform(jax.random.fold_in(jax.random.fold_in(rng, 6), axis_at), (shards_of,), jnp.float32, low / len(split), largest / len(split))
        return jnp.repeat(jnp.exp(heights), shape[axis_at] // shards_of).reshape((-1,) + (1,) * (len(shape) - axis_at - 1))

    loudness = one(*split[0])
    for cut in split[1:]:
        loudness = loudness * one(*cut)
    return loudness


def noise(own_key, dims, deviation, most, shards=(), dtype=jnp.bfloat16):
    values = jax.random.normal(own_key, dims, jnp.float32) * deviation
    if len(shards) > 0:
        values = shard_levels(own_key, dims, shards, -0.22, 0.18) * values
    return jnp.clip(values, min=-most, max=most).astype(dtype)


def setup_inputs(seed: int = 0) -> dict:
    splits = jax.random.split(jax.random.key(seed), 7)
    return {
        "forward_state": noise(splits[0], (SEGMENTS, 2, HEIGHT, TILE_COLS, CHANNELS), 1.0, 6.0, ((0, 8), (2, 4))),
        "returning_state": noise(splits[1], (SEGMENTS, 2, HEIGHT, TILE_COLS, CHANNELS), 1.0, 6.0, ((0, 8), (2, 4))),
        "returning_grad": noise(splits[2], (SEGMENTS, 2, HEIGHT, TILE_COLS, CHANNELS), 1.0, 6.0, ((0, 8), (2, 4))),
        "weights": noise(splits[3], (SEGMENTS, 2, 9 * CHANNELS, CHANNELS), (9 * CHANNELS) ** -0.5, 0.125, ((0, 8),)),
        "fresh_input": noise(splits[4], (TICK_COUNT, 2, HEIGHT, TILE_COLS, CHANNELS), 1.0, 6.0, ((2, 4),)),
        "loss_grad": noise(splits[5], (TICK_COUNT, 2, HEIGHT, TILE_COLS, CHANNELS), 1.0, 6.0, ((2, 4),)),
    }


def activate(values):
    return jax.nn.silu(values.astype(jnp.float32)).astype(jnp.bfloat16)


def silu_slope(values):
    sigmoid = jax.nn.sigmoid(values)
    return sigmoid * (1.0 + values * (1.0 - sigmoid))


def rows_padded(field):
    return jnp.pad(field, ((1, 1), (0, 0), (0, 0)))


def gather_taps(rowpadded, flipped):
    height = rowpadded.shape[0] - 2
    across = rowpadded.shape[1]
    padded = jnp.pad(rowpadded, ((0, 0), (1, 1), (0, 0)))
    pieces = []
    for first in range(3):
        for second in range(3):
            if flipped:
                row_start, col_start = 2 - first, 2 - second
            else:
                row_start, col_start = first, second
            pieces.append(padded[row_start:row_start + height, col_start:col_start + across, :])
    return jnp.concatenate(pieces, -1).reshape(height * across, -1)


def apply_taps(taps_matrix, weight):
    return jnp.dot(taps_matrix, weight, preferred_element_type=jnp.float32)


def flip_weight(weight, channels):
    return weight.reshape(9, channels, channels).transpose(0, 2, 1).reshape(9 * channels, channels)


def correlate(taps_matrix, grads):
    return lax.dot_general(taps_matrix, grads, (((0,), (0,)), ((), ())), preferred_element_type=jnp.float32)


def forward_block(inputs, weight_f, weight_g):
    first_in, second_in = inputs[0], inputs[1]
    shape = first_in.shape
    taps_f = gather_taps(rows_padded(activate(second_in)), False)
    first_out = (first_in.astype(jnp.float32) + apply_taps(taps_f, weight_f).reshape(shape)).astype(jnp.bfloat16)
    taps_g = gather_taps(rows_padded(activate(first_out)), False)
    second_out = (second_in.astype(jnp.float32) + apply_taps(taps_g, weight_g).reshape(shape)).astype(jnp.bfloat16)
    return jnp.stack([first_out, second_out])


def backward_block(outputs, grads, weight_f, weight_g):
    first_out, second_out = outputs[0], outputs[1]
    first_grad, second_grad = grads[0], grads[1]
    shape = first_out.shape
    channels = shape[2]
    taps_g = gather_taps(rows_padded(activate(first_out)), False)
    second_in = (second_out.astype(jnp.float32) - apply_taps(taps_g, weight_g).reshape(shape)).astype(jnp.bfloat16)
    taps_f = gather_taps(rows_padded(activate(second_in)), False)
    first_in = (first_out.astype(jnp.float32) - apply_taps(taps_f, weight_f).reshape(shape)).astype(jnp.bfloat16)
    back_g = apply_taps(gather_taps(rows_padded(second_grad), True), flip_weight(weight_g, channels)).reshape(shape)
    first_back = (first_grad.astype(jnp.float32) + silu_slope(first_out.astype(jnp.float32)) * back_g).astype(jnp.bfloat16)
    back_f = apply_taps(gather_taps(rows_padded(first_back), True), flip_weight(weight_f, channels)).reshape(shape)
    second_back = (second_grad.astype(jnp.float32) + silu_slope(second_in.astype(jnp.float32)) * back_f).astype(jnp.bfloat16)
    grad_f = correlate(taps_f, first_back.reshape(-1, channels))
    grad_g = correlate(taps_g, second_grad.reshape(-1, channels))
    return jnp.stack([first_in, second_in]), jnp.stack([first_back, second_back]), jnp.stack([grad_f, grad_g])


def one_segment(pieces):
    state, outputs, grads, weight = pieces
    advanced = forward_block(state, weight[0], weight[1])
    inverted, backed, wgrad = backward_block(outputs, grads, weight[0], weight[1])
    return advanced, inverted, backed, wgrad


def reference(forward_state, returning_state, returning_grad, weights, fresh_input, loss_grad):
    totals = jnp.zeros((SEGMENTS, 2, 9 * CHANNELS, CHANNELS), jnp.float32)
    for tick_index in range(TICK_COUNT):
        advanced, inverted, backed, wgrad = lax.map(one_segment, (forward_state, returning_state, returning_grad, weights))
        totals = totals + wgrad
        forward_state = jnp.concatenate([fresh_input[tick_index][None], advanced[:-1]], 0)
        returning_state = jnp.concatenate([inverted[1:], advanced[-1:]], 0)
        returning_grad = jnp.concatenate([backed[1:], loss_grad[tick_index][None]], 0)
    return forward_state, returning_state, returning_grad, totals
```

```python
import functools

import jax
import jax.numpy as jnp
from jax import lax
from jax.experimental import pallas as pl
from jax.experimental.pallas import tpu as pltpu
from jax.sharding import PartitionSpec as P

MESH = pl.DeviceIdType.MESH
ACT_Q, ACT_OUT, ACT_Y, GRAD2, ACT_IN, BACK1 = range(6)
FWD1, FWD2, RET1, RET2, GRD1, GRD2 = range(6)


def kernel(ticks, segments, bands, width, fwd_in, ret_in, grd_in, weights_in, fresh_in, loss_in,
           fwd_out, ret_out, grd_out, wgrad_out,
           fwd_v, ret_v, grd_v, wts, flipped, stack, halo_src, halo_dst, sent, came, total, total_half, partial,
           in_sem, edge_sem, halo_send, halo_recv, move_send, move_recv, red_send, red_recv):
    seg = lax.axis_index("segment")
    band = lax.axis_index("band")
    pixels = fwd_v.shape[1]
    channels = fwd_v.shape[2]
    triple = 3 * channels
    chunk = partial.shape[2]
    first_seg, last_seg = seg == 0, seg == segments - 1

    loads = [
        pltpu.make_async_copy(fwd_in, fwd_v, in_sem.at[0]),
        pltpu.make_async_copy(ret_in, ret_v, in_sem.at[1]),
        pltpu.make_async_copy(grd_in, grd_v, in_sem.at[2]),
        pltpu.make_async_copy(weights_in.at[0], wts.at[0], in_sem.at[3]),
        pltpu.make_async_copy(weights_in.at[1], wts.at[1], in_sem.at[4]),
    ]
    for load in loads:
        load.start()

    barrier = pltpu.get_barrier_semaphore()
    for step in range(1, bands):
        pl.semaphore_signal(barrier, inc=1, device_id=(seg, lax.rem(band + step, bands)), device_id_type=MESH)

    @pl.when(seg > 0)
    def _():
        pl.semaphore_signal(barrier, inc=1, device_id=(seg - 1, band), device_id_type=MESH)

    @pl.when(seg < segments - 1)
    def _():
        pl.semaphore_signal(barrier, inc=1, device_id=(seg + 1, band), device_id_type=MESH)

    def landing(tick, field):
        if tick < ticks - 1:
            return came.at[tick, field]
        return (fwd_out, ret_out, grd_out)[field // 2].at[field % 2]

    def edge_copies(tick):
        if tick < ticks - 1:
            targets = (came.at[tick, pl.ds(FWD1, 2)], came.at[tick, pl.ds(GRD1, 2)])
        else:
            targets = (fwd_out, grd_out)
        return (
            pltpu.make_async_copy(fresh_in.at[tick], targets[0], edge_sem.at[tick, 0]),
            pltpu.make_async_copy(loss_in.at[tick], targets[1], edge_sem.at[tick, 1]),
        )

    for tick in range(ticks):
        fresh_copy, loss_copy = edge_copies(tick)
        pl.when(first_seg)(fresh_copy.start)
        pl.when(last_seg)(loss_copy.start)

    column = lax.rem(lax.broadcasted_iota(jnp.int32, (pixels, channels), 0), width)
    at_left, at_right = column == 0, column == width - 1

    def fill(field, start, value):
        rows = value.shape[0]
        wide = value.astype(jnp.float32)
        left = jnp.where(at_left[:rows], 0.0, pltpu.roll(wide, 1, 0))
        right = jnp.where(at_right[:rows], 0.0, pltpu.roll(wide, rows - 1, 0))
        stack[field, start:start + rows, 0:channels] = left.astype(jnp.bfloat16)
        stack[field, start:start + rows, channels:2 * channels] = value
        stack[field, start:start + rows, 2 * channels:triple] = right.astype(jnp.bfloat16)

    def halo_copy(tick, field, side):
        return pltpu.make_async_remote_copy(
            src_ref=halo_src.at[tick, field, side], dst_ref=halo_dst.at[tick, field, 1 - side],
            send_sem=halo_send.at[tick, field, side], recv_sem=halo_recv.at[tick, field, 1 - side],
            device_id=(seg, band - 1 if side == 0 else band + 1), device_id_type=MESH)

    def prepare(tick, field, value):
        halo_src[tick, field, 0] = value[:width]
        halo_src[tick, field, 1] = value[pixels - width:]

    def send_halo(tick, field):
        pl.when(band > 0)(halo_copy(tick, field, 0).start)
        pl.when(band < bands - 1)(halo_copy(tick, field, 1).start)

    def take_halo(tick, field):
        zero = jnp.zeros((width, triple), jnp.bfloat16)

        @pl.when(band > 0)
        def _():
            halo_copy(tick, field, 1).wait_recv()
            fill(field, 0, halo_dst[tick, field, 0])

        @pl.when(band == 0)
        def _():
            stack[field, 0:width] = zero

        @pl.when(band < bands - 1)
        def _():
            halo_copy(tick, field, 0).wait_recv()
            fill(field, pixels + width, halo_dst[tick, field, 1])

        @pl.when(band == bands - 1)
        def _():
            stack[field, pixels + width:pixels + 2 * width] = zero

    def apply(field, kernel_ref):
        result = None
        for row in range(3):
            term = jnp.dot(stack[field, row * width:row * width + pixels],
                           kernel_ref[row * triple:(row + 1) * triple],
                           preferred_element_type=jnp.float32)
            result = term if result is None else result + term
        return result

    def correlate(tick, index, field, grads):
        for row in range(3):
            term = lax.dot_general(stack[field, row * width:row * width + pixels], grads,
                                   (((0,), (0,)), ((), ())), preferred_element_type=jnp.float32)
            rows = slice(row * triple, (row + 1) * triple)
            if tick > 0:
                term = total[index, rows] + term
            total[index, rows] = term
            if tick == ticks - 1:
                total_half[index, rows] = term.astype(jnp.bfloat16)

    def flip(index):
        for tap in range(9):
            back = 8 - tap
            flipped[index, tap * channels:(tap + 1) * channels] = (
                wts[index, back * channels:(back + 1) * channels].T)

    def act(value):
        wide = value.astype(jnp.float32)
        return (wide * jax.nn.sigmoid(wide)).astype(jnp.bfloat16)

    def slope(value):
        wide = value.astype(jnp.float32)
        sigmoid = jax.nn.sigmoid(wide)
        return sigmoid * (1.0 + wide * (1.0 - sigmoid))

    def move_copy(tick, field):
        other = seg + 1 if field < RET1 else seg - 1
        return pltpu.make_async_remote_copy(
            src_ref=sent.at[tick, field], dst_ref=landing(tick, field),
            send_sem=move_send.at[tick, field], recv_sem=move_recv.at[tick, field],
            device_id=(other, band), device_id_type=MESH)

    def send_on(tick, field, value):
        sent[tick, field] = value
        if field < RET1:
            pl.when(seg < segments - 1)(move_copy(tick, field).start)

            @pl.when(last_seg)
            def _():
                landing(tick, field + RET1)[...] = value
        else:
            pl.when(seg > 0)(move_copy(tick, field).start)

    def take(tick, fields):
        for field in fields:
            if field < RET1:
                pl.when(seg > 0)(move_copy(tick, field).wait_recv)
            else:
                pl.when(seg < segments - 1)(move_copy(tick, field).wait_recv)
        fresh_copy, loss_copy = edge_copies(tick)
        if FWD1 in fields:
            pl.when(first_seg)(fresh_copy.wait)
        if GRD1 in fields:
            pl.when(last_seg)(loss_copy.wait)

    def reduce_copy(step, index):
        other = lax.rem(band + step, bands)
        rows = pl.ds(pl.multiple_of(other * chunk, chunk), chunk)
        return pltpu.make_async_remote_copy(
            src_ref=total_half.at[index, rows], dst_ref=partial.at[step - 1, index],
            send_sem=red_send.at[step - 1, index], recv_sem=red_recv.at[step - 1, index],
            device_id=(seg, other), device_id_type=MESH)

    def send_sums(index):
        for step in range(1, bands):
            reduce_copy(step, index).start()

    def begin(tick, field, value):
        prepare(tick, field, value)
        if tick == 0 and not entered:
            waiting.append(field)
        else:
            send_halo(tick, field)
        fill(field, width, value)

    entered, waiting = [], []
    for tick in range(ticks):
        if tick == 0:
            p, q = fwd_v.at[0], fwd_v.at[1]
            y1, y2 = ret_v.at[0], ret_v.at[1]
            g1, g2 = grd_v.at[0], grd_v.at[1]
            loads[0].wait()
        else:
            p, q, y1, y2, g1, g2 = (came.at[tick - 1, field] for field in range(6))
            take(tick - 1, (FWD1, FWD2))
        begin(tick, ACT_Q, act(q[...]))
        if tick == 0:
            loads[1].wait()
            begin(tick, ACT_Y, act(y1[...]))
            loads[2].wait()
            begin(tick, GRAD2, g2[...])
            others = (seg > 0).astype(jnp.int32) + (seg < segments - 1).astype(jnp.int32)
            pl.semaphore_wait(barrier, bands - 1 + others)
            entered.append(True)
            for field in waiting:
                send_halo(tick, field)
            loads[3].wait()

        def advance_first():
            take_halo(tick, ACT_Q)
            out1 = (p[...].astype(jnp.float32) + apply(ACT_Q, wts.at[0])).astype(jnp.bfloat16)
            send_on(tick, FWD1, out1)
            begin(tick, ACT_OUT, act(out1))

        def advance_second():
            take_halo(tick, ACT_OUT)
            out2 = (q[...].astype(jnp.float32) + apply(ACT_OUT, wts.at[1])).astype(jnp.bfloat16)
            send_on(tick, FWD2, out2)

        advance_first()
        if tick == 0:
            loads[4].wait()
        else:
            advance_second()
            take(tick - 1, (RET1, RET2, GRD1, GRD2))
            begin(tick, ACT_Y, act(y1[...]))
            begin(tick, GRAD2, g2[...])
        take_halo(tick, ACT_Y)
        q2 = (y2[...].astype(jnp.float32) - apply(ACT_Y, wts.at[1])).astype(jnp.bfloat16)
        send_on(tick, RET2, q2)
        begin(tick, ACT_IN, act(q2))
        take_halo(tick, GRAD2)
        if tick == 0:
            flip(1)
        h1 = (g1[...].astype(jnp.float32) + slope(y1[...]) * apply(GRAD2, flipped.at[1])).astype(jnp.bfloat16)
        send_on(tick, GRD1, h1)
        begin(tick, BACK1, h1)
        if tick == 0:
            advance_second()
            flip(0)
        take_halo(tick, ACT_IN)
        p2 = (y1[...].astype(jnp.float32) - apply(ACT_IN, wts.at[0])).astype(jnp.bfloat16)
        send_on(tick, RET1, p2)
        take_halo(tick, BACK1)
        h2 = (g2[...].astype(jnp.float32)
              + slope(sent[tick, RET2]) * apply(BACK1, flipped.at[0])).astype(jnp.bfloat16)
        send_on(tick, GRD2, h2)
        correlate(tick, 1, ACT_Y, g2[...])
        if tick == ticks - 1:
            send_sums(1)
        correlate(tick, 0, ACT_IN, sent[tick, GRD1])
        if tick == ticks - 1:
            send_sums(0)

    own = pl.ds(pl.multiple_of(band * chunk, chunk), chunk)
    for index in (1, 0):
        for step in range(1, bands):
            reduce_copy(step, index).wait_recv()
        value = total[index, own]
        for step in range(1, bands):
            value = value + partial[step - 1, index].astype(jnp.float32)
        wgrad_out[index] = value
    take(ticks - 1, range(6))
    for index in (1, 0):
        for step in range(1, bands):
            reduce_copy(step, index).wait_send()
    for tick in range(ticks):
        for field in range(6):
            pl.when(band > 0)(halo_copy(tick, field, 0).wait_send)
            pl.when(band < bands - 1)(halo_copy(tick, field, 1).wait_send)
            if field < RET1:
                pl.when(seg < segments - 1)(move_copy(tick, field).wait_send)
            else:
                pl.when(seg > 0)(move_copy(tick, field).wait_send)


def local(forward_state, returning_state, returning_grad, weights, fresh_input, loss_grad):
    segments, bands = lax.axis_size("segment"), lax.axis_size("band")
    _, _, rows, width, channels = forward_state.shape
    pixels = rows * width
    ticks = fresh_input.shape[0]
    taps = weights.shape[2]
    chunk = taps // bands
    bf16, f32 = jnp.bfloat16, jnp.float32
    pair = jax.ShapeDtypeStruct((2, pixels, channels), bf16)
    dma = pltpu.SemaphoreType.DMA
    flat = lambda x: x.reshape(x.shape[:-3] + (pixels, channels))
    vmem = pl.BlockSpec(memory_space=pltpu.VMEM)
    outs = pl.pallas_call(
        functools.partial(kernel, ticks, segments, bands, width),
        out_shape=(pair, pair, pair, jax.ShapeDtypeStruct((2, chunk, channels), f32)),
        in_specs=[pl.BlockSpec(memory_space=pl.ANY)] * 6,
        out_specs=(vmem,) * 4,
        scratch_shapes=[
            pltpu.VMEM((2, pixels, channels), bf16),
            pltpu.VMEM((2, pixels, channels), bf16),
            pltpu.VMEM((2, pixels, channels), bf16),
            pltpu.VMEM((2, taps, channels), bf16),
            pltpu.VMEM((2, taps, channels), bf16),
            pltpu.VMEM((6, pixels + 2 * width, 3 * channels), bf16),
            pltpu.VMEM((ticks, 6, 2, width, channels), bf16),
            pltpu.VMEM((ticks, 6, 2, width, channels), bf16),
            pltpu.VMEM((ticks, 6, pixels, channels), bf16),
            pltpu.VMEM((max(ticks - 1, 1), 6, pixels, channels), bf16),
            pltpu.VMEM((2, taps, channels), f32),
            pltpu.VMEM((2, taps, channels), bf16),
            pltpu.VMEM((bands - 1, 2, chunk, channels), bf16),
            dma((5,)),
            dma((ticks, 2)),
            dma((ticks, 6, 2)),
            dma((ticks, 6, 2)),
            dma((ticks, 6)),
            dma((ticks, 6)),
            dma((bands - 1, 2)),
            dma((bands - 1, 2)),
        ],
        compiler_params=pltpu.CompilerParams(
            collective_id=0, has_side_effects=True, vmem_limit_bytes=60 * 2**20),
    )(flat(forward_state[0]), flat(returning_state[0]), flat(returning_grad[0]), weights[0],
      flat(fresh_input), flat(loss_grad))
    shape = forward_state.shape
    return tuple(o.reshape(shape) for o in outs[:3]) + (outs[3][None],)


def solution(mesh):
    pair = P("segment", None, "band", None, None)
    whole = P(None, None, "band", None, None)
    return jax.shard_map(
        local,
        mesh=mesh,
        in_specs=(pair, pair, pair, P("segment", None, None, None), whole, whole),
        out_specs=(pair, pair, pair, P("segment", None, "band", None)),
        check_vma=False,
    )
```

```python
import functools

import jax
import jax.numpy as jnp
from jax import lax
from jax.experimental import pallas as pl
from jax.experimental.pallas import tpu as pltpu
from jax.sharding import PartitionSpec as P

MESH = pl.DeviceIdType.MESH
ACT_Q, ACT_OUT, ACT_Y, GRAD2, ACT_IN, BACK1 = range(6)
FWD1, FWD2, RET1, RET2, GRD1, GRD2 = range(6)


def kernel(ticks, segments, bands, width, fwd_in, ret_in, grd_in, weights_in, fresh_in, loss_in,
           fwd_out, ret_out, grd_out, wgrad_out,
           fwd_v, ret_v, grd_v, wts, flipped, stack, halo_src, halo_dst, sent, came, total, total_half, paired, reduced, partial,
           in_sem, edge_sem, halo_send, halo_recv, move_send, move_recv, pair_send, pair_recv,
           red_send, red_recv):
    seg = lax.axis_index("segment")
    band = lax.axis_index("band")
    pixels = fwd_v.shape[1]
    channels = fwd_v.shape[2]
    triple = 3 * channels
    chunk = partial.shape[2]
    first_seg, last_seg = seg == 0, seg == segments - 1

    loads = [
        pltpu.make_async_copy(fwd_in, fwd_v, in_sem.at[0]),
        pltpu.make_async_copy(ret_in, ret_v, in_sem.at[1]),
        pltpu.make_async_copy(grd_in, grd_v, in_sem.at[2]),
        pltpu.make_async_copy(weights_in.at[0], wts.at[0], in_sem.at[3]),
        pltpu.make_async_copy(weights_in.at[1], wts.at[1], in_sem.at[4]),
    ]
    for load in loads:
        load.start()

    barrier = pltpu.get_barrier_semaphore()
    for step in range(1, bands):
        pl.semaphore_signal(barrier, inc=1, device_id=(seg, lax.rem(band + step, bands)), device_id_type=MESH)

    @pl.when(seg > 0)
    def _():
        pl.semaphore_signal(barrier, inc=1, device_id=(seg - 1, band), device_id_type=MESH)

    @pl.when(seg < segments - 1)
    def _():
        pl.semaphore_signal(barrier, inc=1, device_id=(seg + 1, band), device_id_type=MESH)

    def landing(tick, field):
        if tick < ticks - 1:
            return came.at[tick, field]
        return (fwd_out, ret_out, grd_out)[field // 2].at[field % 2]

    def edge_copies(tick):
        if tick < ticks - 1:
            targets = (came.at[tick, pl.ds(FWD1, 2)], came.at[tick, pl.ds(GRD1, 2)])
        else:
            targets = (fwd_out, grd_out)
        return (
            pltpu.make_async_copy(fresh_in.at[tick], targets[0], edge_sem.at[tick, 0]),
            pltpu.make_async_copy(loss_in.at[tick], targets[1], edge_sem.at[tick, 1]),
        )

    for tick in range(ticks):
        fresh_copy, loss_copy = edge_copies(tick)
        pl.when(first_seg)(fresh_copy.start)
        pl.when(last_seg)(loss_copy.start)

    column = lax.rem(lax.broadcasted_iota(jnp.int32, (pixels, channels), 0), width)
    at_left, at_right = column == 0, column == width - 1

    def fill(field, start, value):
        rows = value.shape[0]
        wide = value.astype(jnp.float32)
        left = jnp.where(at_left[:rows], 0.0, pltpu.roll(wide, 1, 0))
        right = jnp.where(at_right[:rows], 0.0, pltpu.roll(wide, rows - 1, 0))
        stack[field, start:start + rows, 0:channels] = left.astype(jnp.bfloat16)
        stack[field, start:start + rows, channels:2 * channels] = value
        stack[field, start:start + rows, 2 * channels:triple] = right.astype(jnp.bfloat16)

    def halo_copy(tick, field, side):
        return pltpu.make_async_remote_copy(
            src_ref=halo_src.at[tick, field, side], dst_ref=halo_dst.at[tick, field, 1 - side],
            send_sem=halo_send.at[tick, field, side], recv_sem=halo_recv.at[tick, field, 1 - side],
            device_id=(seg, band - 1 if side == 0 else band + 1), device_id_type=MESH)

    def send_halo(tick, field):
        pl.when(band > 0)(halo_copy(tick, field, 0).start)
        pl.when(band < bands - 1)(halo_copy(tick, field, 1).start)

    def take_halo(tick, field):
        zero = jnp.zeros((width, triple), jnp.bfloat16)

        @pl.when(band > 0)
        def _():
            halo_copy(tick, field, 1).wait_recv()
            fill(field, 0, halo_dst[tick, field, 0])

        @pl.when(band == 0)
        def _():
            stack[field, 0:width] = zero

        @pl.when(band < bands - 1)
        def _():
            halo_copy(tick, field, 0).wait_recv()
            fill(field, pixels + width, halo_dst[tick, field, 1])

        @pl.when(band == bands - 1)
        def _():
            stack[field, pixels + width:pixels + 2 * width] = zero

    def apply(field, kernel_ref):
        result = None
        for row in range(3):
            term = jnp.dot(stack[field, row * width:row * width + pixels],
                           kernel_ref[row * triple:(row + 1) * triple],
                           preferred_element_type=jnp.float32)
            result = term if result is None else result + term
        return result

    def correlate(tick, index, field, grads):
        for row in range(3):
            term = lax.dot_general(stack[field, row * width:row * width + pixels], grads,
                                   (((0,), (0,)), ((), ())), preferred_element_type=jnp.float32)
            rows = slice(row * triple, (row + 1) * triple)
            if tick > 0:
                term = total[index, rows] + term
            total[index, rows] = term
            if tick == ticks - 1:
                total_half[index, rows] = term.astype(jnp.bfloat16)

    def flip(index):
        for tap in range(9):
            back = 8 - tap
            flipped[index, tap * channels:(tap + 1) * channels] = (
                wts[index, back * channels:(back + 1) * channels].T)

    def act(value):
        wide = value.astype(jnp.float32)
        return (wide * jax.nn.sigmoid(wide)).astype(jnp.bfloat16)

    def slope(value):
        wide = value.astype(jnp.float32)
        sigmoid = jax.nn.sigmoid(wide)
        return sigmoid * (1.0 + wide * (1.0 - sigmoid))

    def move_copy(tick, field):
        other = seg + 1 if field < RET1 else seg - 1
        return pltpu.make_async_remote_copy(
            src_ref=sent.at[tick, field], dst_ref=landing(tick, field),
            send_sem=move_send.at[tick, field], recv_sem=move_recv.at[tick, field],
            device_id=(other, band), device_id_type=MESH)

    def send_on(tick, field, value):
        sent[tick, field] = value
        if field < RET1:
            pl.when(seg < segments - 1)(move_copy(tick, field).start)

            @pl.when(last_seg)
            def _():
                landing(tick, field + RET1)[...] = value
        else:
            pl.when(seg > 0)(move_copy(tick, field).start)

    def take(tick, fields):
        for field in fields:
            if field < RET1:
                pl.when(seg > 0)(move_copy(tick, field).wait_recv)
            else:
                pl.when(seg < segments - 1)(move_copy(tick, field).wait_recv)
        fresh_copy, loss_copy = edge_copies(tick)
        if FWD1 in fields:
            pl.when(first_seg)(fresh_copy.wait)
        if GRD1 in fields:
            pl.when(last_seg)(loss_copy.wait)

    groups = bands // 2
    core, group = lax.rem(band, 2), band // 2

    def chunk_rows(owner):
        return pl.ds(pl.multiple_of(owner * chunk, chunk), chunk)

    def pair_copy(index, target):
        return pltpu.make_async_remote_copy(
            src_ref=total_half.at[index, chunk_rows(2 * target + 1 - core)], dst_ref=paired.at[index, target],
            send_sem=pair_send.at[index, target], recv_sem=pair_recv.at[index, target],
            device_id=(seg, band + 1 - 2 * core), device_id_type=MESH)

    def reduce_copy(index, step):
        other = 2 * lax.rem(group + step, groups) + core
        return pltpu.make_async_remote_copy(
            src_ref=reduced.at[index, step - 1], dst_ref=partial.at[index, step - 1],
            send_sem=red_send.at[index, step - 1], recv_sem=red_recv.at[index, step - 1],
            device_id=(seg, other), device_id_type=MESH)

    def start_sums(index):
        for target in range(groups):
            pair_copy(index, target).start()

    def pair_sum(index, target):
        return total[index, chunk_rows(2 * target + core)] + paired[index, target].astype(jnp.float32)

    def pass_sums(index):
        for target in range(groups):
            pair_copy(index, target).wait_recv()
        for step in range(1, groups):
            reduced[index, step - 1] = pair_sum(index, lax.rem(group + step, groups)).astype(jnp.bfloat16)
            reduce_copy(index, step).start()

    def finish_sums(index):
        value = pair_sum(index, group)
        for step in range(1, groups):
            reduce_copy(index, step).wait_recv()
            value = value + partial[index, step - 1].astype(jnp.float32)
        wgrad_out[index] = value

    def begin(tick, field, ref, function):
        halo_src[tick, field, 0] = function(ref[0:width])
        halo_src[tick, field, 1] = function(ref[pixels - width:pixels])
        send_halo(tick, field)
        fill(field, width, function(ref[...]))

    for tick in range(ticks):
        last_tick = tick == ticks - 1
        if tick == 0:
            p, q = fwd_v.at[0], fwd_v.at[1]
            y1, y2 = ret_v.at[0], ret_v.at[1]
            g1, g2 = grd_v.at[0], grd_v.at[1]
        else:
            p, q, y1, y2, g1, g2 = (came.at[tick - 1, field] for field in range(6))

        def same(value):
            return value

        def advance_first():
            take_halo(tick, ACT_Q)
            out1 = (p[...].astype(jnp.float32) + apply(ACT_Q, wts.at[0])).astype(jnp.bfloat16)
            send_on(tick, FWD1, out1)
            begin(tick, ACT_OUT, sent.at[tick, FWD1], act)

        def advance_second():
            take_halo(tick, ACT_OUT)
            out2 = (q[...].astype(jnp.float32) + apply(ACT_OUT, wts.at[1])).astype(jnp.bfloat16)
            send_on(tick, FWD2, out2)

        def invert_second():
            take_halo(tick, ACT_Y)
            q2 = (y2[...].astype(jnp.float32) - apply(ACT_Y, wts.at[1])).astype(jnp.bfloat16)
            send_on(tick, RET2, q2)
            begin(tick, ACT_IN, sent.at[tick, RET2], act)

        def invert_first():
            take_halo(tick, ACT_IN)
            p2 = (y1[...].astype(jnp.float32) - apply(ACT_IN, wts.at[0])).astype(jnp.bfloat16)
            send_on(tick, RET1, p2)

        def back_first():
            take_halo(tick, GRAD2)
            h1 = (g1[...].astype(jnp.float32) + slope(y1[...]) * apply(GRAD2, flipped.at[1])).astype(jnp.bfloat16)
            send_on(tick, GRD1, h1)
            begin(tick, BACK1, sent.at[tick, GRD1], same)

        def back_second():
            take_halo(tick, BACK1)
            h2 = (g2[...].astype(jnp.float32)
                  + slope(sent[tick, RET2]) * apply(BACK1, flipped.at[0])).astype(jnp.bfloat16)
            send_on(tick, GRD2, h2)

        if tick == 0:
            loads[0].wait()
            others = (seg > 0).astype(jnp.int32) + (seg < segments - 1).astype(jnp.int32)
            pl.semaphore_wait(barrier, bands - 1 + others)
            begin(tick, ACT_Q, q, act)
            loads[1].wait()
            begin(tick, ACT_Y, y1, act)
            loads[3].wait()
            advance_first()
            loads[2].wait()
            begin(tick, GRAD2, g2, same)
            loads[4].wait()
            invert_second()
            advance_second()
            flip(1)
            back_first()
            invert_first()
            flip(0)
            back_second()
        else:
            take(tick - 1, (FWD1, FWD2))
            begin(tick, ACT_Q, q, act)
            advance_first()
            advance_second()
            take(tick - 1, (RET1, RET2))
            begin(tick, ACT_Y, y1, act)
            invert_second()
            take(tick - 1, (GRD1, GRD2))
            begin(tick, GRAD2, g2, same)
            back_first()
        correlate(tick, 1, ACT_Y, g2[...])
        if last_tick:
            start_sums(1)
        if tick > 0:
            invert_first()
        correlate(tick, 0, ACT_IN, sent[tick, GRD1])
        if last_tick:
            start_sums(0)
        if tick > 0:
            back_second()
        if last_tick:
            pass_sums(1)
            pass_sums(0)

    finish_sums(1)
    finish_sums(0)
    take(ticks - 1, range(6))
    for index in range(2):
        for target in range(groups):
            pair_copy(index, target).wait_send()
        for step in range(1, groups):
            reduce_copy(index, step).wait_send()
    for tick in range(ticks):
        for field in range(6):
            pl.when(band > 0)(halo_copy(tick, field, 0).wait_send)
            pl.when(band < bands - 1)(halo_copy(tick, field, 1).wait_send)
            if field < RET1:
                pl.when(seg < segments - 1)(move_copy(tick, field).wait_send)
            else:
                pl.when(seg > 0)(move_copy(tick, field).wait_send)


def store(*refs):
    count = len(refs) // 2
    sems = refs[-1]
    copies = [pltpu.make_async_copy(refs[i], refs[count + i], sems.at[i]) for i in range(count)]
    for copy in copies:
        copy.start()
    for copy in copies:
        copy.wait()


def local(forward_state, returning_state, returning_grad, weights, fresh_input, loss_grad):
    segments, bands = lax.axis_size("segment"), lax.axis_size("band")
    _, _, rows, width, channels = forward_state.shape
    pixels = rows * width
    ticks = fresh_input.shape[0]
    taps = weights.shape[2]
    chunk = taps // bands
    bf16, f32 = jnp.bfloat16, jnp.float32
    pair = jax.ShapeDtypeStruct((2, pixels, channels), bf16)
    dma = pltpu.SemaphoreType.DMA
    flat = lambda x: x.reshape(x.shape[:-3] + (pixels, channels))
    vmem = pl.BlockSpec(memory_space=pltpu.VMEM)
    outs = pl.pallas_call(
        functools.partial(kernel, ticks, segments, bands, width),
        out_shape=(pair, pair, pair, jax.ShapeDtypeStruct((2, chunk, channels), f32)),
        in_specs=[pl.BlockSpec(memory_space=pl.ANY)] * 6,
        out_specs=(vmem,) * 4,
        scratch_shapes=[
            pltpu.VMEM((2, pixels, channels), bf16),
            pltpu.VMEM((2, pixels, channels), bf16),
            pltpu.VMEM((2, pixels, channels), bf16),
            pltpu.VMEM((2, taps, channels), bf16),
            pltpu.VMEM((2, taps, channels), bf16),
            pltpu.VMEM((6, pixels + 2 * width, 3 * channels), bf16),
            pltpu.VMEM((ticks, 6, 2, width, channels), bf16),
            pltpu.VMEM((ticks, 6, 2, width, channels), bf16),
            pltpu.VMEM((ticks, 6, pixels, channels), bf16),
            pltpu.VMEM((max(ticks - 1, 1), 6, pixels, channels), bf16),
            pltpu.VMEM((2, taps, channels), f32),
            pltpu.VMEM((2, taps, channels), bf16),
            pltpu.VMEM((2, bands // 2, chunk, channels), bf16),
            pltpu.VMEM((2, bands // 2 - 1, chunk, channels), bf16),
            pltpu.VMEM((2, bands // 2 - 1, chunk, channels), bf16),
            dma((5,)),
            dma((ticks, 2)),
            dma((ticks, 6, 2)),
            dma((ticks, 6, 2)),
            dma((ticks, 6)),
            dma((ticks, 6)),
            dma((2, bands // 2)),
            dma((2, bands // 2)),
            dma((2, bands // 2 - 1)),
            dma((2, bands // 2 - 1)),
        ],
        compiler_params=pltpu.CompilerParams(
            collective_id=0, has_side_effects=True, vmem_limit_bytes=60 * 2**20),
    )(flat(forward_state[0]), flat(returning_state[0]), flat(returning_grad[0]), weights[0],
      flat(fresh_input), flat(loss_grad))
    outs = pl.pallas_call(
        store,
        out_shape=tuple(jax.ShapeDtypeStruct(o.shape, o.dtype) for o in outs),
        in_specs=[vmem] * 4,
        out_specs=(pl.BlockSpec(memory_space=pl.ANY),) * 4,
        scratch_shapes=[dma((4,))],
    )(*outs)
    shape = forward_state.shape
    return tuple(o.reshape(shape) for o in outs[:3]) + (outs[3][None],)


def solution(mesh):
    pair = P("segment", None, "band", None, None)
    whole = P(None, None, "band", None, None)
    return jax.shard_map(
        local,
        mesh=mesh,
        in_specs=(pair, pair, pair, P("segment", None, None, None), whole, whole),
        out_specs=(pair, pair, pair, P("segment", None, "band", None)),
        check_vma=False,
    )
```

```python
import functools

import jax
import jax.numpy as jnp
from jax import lax
from jax.experimental import pallas as pl
from jax.experimental.pallas import tpu as pltpu
from jax.sharding import PartitionSpec as P

MESH = pl.DeviceIdType.MESH
ACT_Q, ACT_OUT, ACT_Y, GRAD2, ACT_IN, BACK1 = range(6)
FWD1, FWD2, RET1, RET2, GRD1, GRD2 = range(6)


def kernel(ticks, segments, bands, width, fwd_in, ret_in, grd_in, weights_in, fresh_in, loss_in,
           fwd_out, ret_out, grd_out, wgrad_out,
           fwd_v, ret_v, grd_v, wts, flipped, stack, halo_src, halo_dst, sent, came, total, total_half, paired, reduced, partial,
           in_sem, edge_sem, halo_send, halo_recv, move_send, move_recv, pair_send, pair_recv,
           red_send, red_recv):
    seg = lax.axis_index("segment")
    band = lax.axis_index("band")
    pixels = fwd_v.shape[1]
    channels = fwd_v.shape[2]
    triple = 3 * channels
    chunk = partial.shape[2]
    first_seg, last_seg = seg == 0, seg == segments - 1

    loads = [
        pltpu.make_async_copy(fwd_in, fwd_v, in_sem.at[0]),
        pltpu.make_async_copy(ret_in, ret_v, in_sem.at[1]),
        pltpu.make_async_copy(grd_in, grd_v, in_sem.at[2]),
        pltpu.make_async_copy(weights_in.at[0], wts.at[0], in_sem.at[3]),
        pltpu.make_async_copy(weights_in.at[1], wts.at[1], in_sem.at[4]),
    ]
    for load in loads:
        load.start()

    barrier = pltpu.get_barrier_semaphore()
    for step in range(1, bands):
        pl.semaphore_signal(barrier, inc=1, device_id=(seg, lax.rem(band + step, bands)), device_id_type=MESH)

    @pl.when(seg > 0)
    def _():
        pl.semaphore_signal(barrier, inc=1, device_id=(seg - 1, band), device_id_type=MESH)

    @pl.when(seg < segments - 1)
    def _():
        pl.semaphore_signal(barrier, inc=1, device_id=(seg + 1, band), device_id_type=MESH)

    def landing(tick, field):
        if tick < ticks - 1:
            return came.at[tick, field]
        return (fwd_out, ret_out, grd_out)[field // 2].at[field % 2]

    def edge_copies(tick):
        if tick < ticks - 1:
            targets = (came.at[tick, pl.ds(FWD1, 2)], came.at[tick, pl.ds(GRD1, 2)])
        else:
            targets = (fwd_out, grd_out)
        return (
            pltpu.make_async_copy(fresh_in.at[tick], targets[0], edge_sem.at[tick, 0]),
            pltpu.make_async_copy(loss_in.at[tick], targets[1], edge_sem.at[tick, 1]),
        )

    for tick in range(ticks):
        fresh_copy, loss_copy = edge_copies(tick)
        pl.when(first_seg)(fresh_copy.start)
        pl.when(last_seg)(loss_copy.start)

    column = lax.rem(lax.broadcasted_iota(jnp.int32, (pixels, channels), 0), width)
    at_left, at_right = column == 0, column == width - 1

    def fill(field, start, value):
        rows = value.shape[0]
        wide = value.astype(jnp.float32)
        left = jnp.where(at_left[:rows], 0.0, pltpu.roll(wide, 1, 0))
        right = jnp.where(at_right[:rows], 0.0, pltpu.roll(wide, rows - 1, 0))
        stack[field, start:start + rows, 0:channels] = left.astype(jnp.bfloat16)
        stack[field, start:start + rows, channels:2 * channels] = value
        stack[field, start:start + rows, 2 * channels:triple] = right.astype(jnp.bfloat16)

    def halo_copy(tick, field, side):
        return pltpu.make_async_remote_copy(
            src_ref=halo_src.at[tick, field, side], dst_ref=halo_dst.at[tick, field, 1 - side],
            send_sem=halo_send.at[tick, field, side], recv_sem=halo_recv.at[tick, field, 1 - side],
            device_id=(seg, band - 1 if side == 0 else band + 1), device_id_type=MESH)

    def send_halo(tick, field):
        pl.when(band > 0)(halo_copy(tick, field, 0).start)
        pl.when(band < bands - 1)(halo_copy(tick, field, 1).start)

    def take_halo(tick, field):
        zero = jnp.zeros((width, triple), jnp.bfloat16)

        @pl.when(band > 0)
        def _():
            halo_copy(tick, field, 1).wait_recv()
            fill(field, 0, halo_dst[tick, field, 0])

        @pl.when(band == 0)
        def _():
            stack[field, 0:width] = zero

        @pl.when(band < bands - 1)
        def _():
            halo_copy(tick, field, 0).wait_recv()
            fill(field, pixels + width, halo_dst[tick, field, 1])

        @pl.when(band == bands - 1)
        def _():
            stack[field, pixels + width:pixels + 2 * width] = zero

    def apply(field, kernel_ref):
        result = None
        for row in range(3):
            term = jnp.dot(stack[field, row * width:row * width + pixels],
                           kernel_ref[row * triple:(row + 1) * triple],
                           preferred_element_type=jnp.float32)
            result = term if result is None else result + term
        return result

    def correlate(tick, index, field, grads):
        for row in range(3):
            term = lax.dot_general(stack[field, row * width:row * width + pixels], grads,
                                   (((0,), (0,)), ((), ())), preferred_element_type=jnp.float32)
            rows = slice(row * triple, (row + 1) * triple)
            if tick > 0:
                term = total[index, rows] + term
            total[index, rows] = term
            if tick == ticks - 1:
                total_half[index, rows] = term.astype(jnp.bfloat16)

    def flip(index):
        for tap in range(9):
            back = 8 - tap
            flipped[index, tap * channels:(tap + 1) * channels] = (
                wts[index, back * channels:(back + 1) * channels].T)

    def act(value):
        wide = value.astype(jnp.float32)
        return (wide * jax.nn.sigmoid(wide)).astype(jnp.bfloat16)

    def slope(value):
        wide = value.astype(jnp.float32)
        sigmoid = jax.nn.sigmoid(wide)
        return sigmoid * (1.0 + wide * (1.0 - sigmoid))

    def move_copy(tick, field):
        other = seg + 1 if field < RET1 else seg - 1
        return pltpu.make_async_remote_copy(
            src_ref=sent.at[tick, field], dst_ref=landing(tick, field),
            send_sem=move_send.at[tick, field], recv_sem=move_recv.at[tick, field],
            device_id=(other, band), device_id_type=MESH)

    def send_on(tick, field, value):
        sent[tick, field] = value
        if field < RET1:
            pl.when(seg < segments - 1)(move_copy(tick, field).start)

            @pl.when(last_seg)
            def _():
                landing(tick, field + RET1)[...] = value
        else:
            pl.when(seg > 0)(move_copy(tick, field).start)

    def take(tick, fields):
        for field in fields:
            if field < RET1:
                pl.when(seg > 0)(move_copy(tick, field).wait_recv)
            else:
                pl.when(seg < segments - 1)(move_copy(tick, field).wait_recv)
        fresh_copy, loss_copy = edge_copies(tick)
        if FWD1 in fields:
            pl.when(first_seg)(fresh_copy.wait)
        if GRD1 in fields:
            pl.when(last_seg)(loss_copy.wait)

    groups = bands // 2
    core, group = lax.rem(band, 2), band // 2

    def chunk_rows(owner):
        return pl.ds(pl.multiple_of(owner * chunk, chunk), chunk)

    def pair_copy(index, target):
        return pltpu.make_async_remote_copy(
            src_ref=total_half.at[index, chunk_rows(2 * target + 1 - core)], dst_ref=paired.at[index, target],
            send_sem=pair_send.at[index, target], recv_sem=pair_recv.at[index, target],
            device_id=(seg, band + 1 - 2 * core), device_id_type=MESH)

    def reduce_copy(index, step):
        other = 2 * lax.rem(group + step, groups) + core
        return pltpu.make_async_remote_copy(
            src_ref=reduced.at[index, step - 1], dst_ref=partial.at[index, step - 1],
            send_sem=red_send.at[index, step - 1], recv_sem=red_recv.at[index, step - 1],
            device_id=(seg, other), device_id_type=MESH)

    def start_sums(index):
        for target in range(groups):
            pair_copy(index, target).start()

    def pair_sum(index, target):
        return total[index, chunk_rows(2 * target + core)] + paired[index, target].astype(jnp.float32)

    def pass_sums(index):
        for target in range(groups):
            pair_copy(index, target).wait_recv()
        for step in range(1, groups):
            reduced[index, step - 1] = pair_sum(index, lax.rem(group + step, groups)).astype(jnp.bfloat16)
            reduce_copy(index, step).start()

    def finish_sums(index):
        value = pair_sum(index, group)
        for step in range(1, groups):
            reduce_copy(index, step).wait_recv()
            value = value + partial[index, step - 1].astype(jnp.float32)
        wgrad_out[index] = value

    def begin(tick, field, ref, function):
        halo_src[tick, field, 0] = function(ref[0:width])
        halo_src[tick, field, 1] = function(ref[pixels - width:pixels])
        send_halo(tick, field)
        fill(field, width, function(ref[...]))

    for tick in range(ticks):
        last_tick = tick == ticks - 1
        if tick == 0:
            p, q = fwd_v.at[0], fwd_v.at[1]
            y1, y2 = ret_v.at[0], ret_v.at[1]
            g1, g2 = grd_v.at[0], grd_v.at[1]
        else:
            p, q, y1, y2, g1, g2 = (came.at[tick - 1, field] for field in range(6))

        def same(value):
            return value

        def advance_first():
            take_halo(tick, ACT_Q)
            out1 = (p[...].astype(jnp.float32) + apply(ACT_Q, wts.at[0])).astype(jnp.bfloat16)
            send_on(tick, FWD1, out1)
            begin(tick, ACT_OUT, sent.at[tick, FWD1], act)

        def advance_second():
            take_halo(tick, ACT_OUT)
            out2 = (q[...].astype(jnp.float32) + apply(ACT_OUT, wts.at[1])).astype(jnp.bfloat16)
            send_on(tick, FWD2, out2)

        def invert_second():
            take_halo(tick, ACT_Y)
            q2 = (y2[...].astype(jnp.float32) - apply(ACT_Y, wts.at[1])).astype(jnp.bfloat16)
            send_on(tick, RET2, q2)
            begin(tick, ACT_IN, sent.at[tick, RET2], act)

        def invert_first():
            take_halo(tick, ACT_IN)
            p2 = (y1[...].astype(jnp.float32) - apply(ACT_IN, wts.at[0])).astype(jnp.bfloat16)
            send_on(tick, RET1, p2)

        def back_first():
            take_halo(tick, GRAD2)
            h1 = (g1[...].astype(jnp.float32) + slope(y1[...]) * apply(GRAD2, flipped.at[1])).astype(jnp.bfloat16)
            send_on(tick, GRD1, h1)
            begin(tick, BACK1, sent.at[tick, GRD1], same)

        def back_second():
            take_halo(tick, BACK1)
            h2 = (g2[...].astype(jnp.float32)
                  + slope(sent[tick, RET2]) * apply(BACK1, flipped.at[0])).astype(jnp.bfloat16)
            send_on(tick, GRD2, h2)

        if tick == 0:
            loads[0].wait()
            others = (seg > 0).astype(jnp.int32) + (seg < segments - 1).astype(jnp.int32)
            pl.semaphore_wait(barrier, bands - 1 + others)
            begin(tick, ACT_Q, q, act)
            loads[1].wait()
            begin(tick, ACT_Y, y1, act)
            loads[3].wait()
            advance_first()
            loads[2].wait()
            begin(tick, GRAD2, g2, same)
            loads[4].wait()
            invert_second()
            advance_second()
            flip(1)
            back_first()
            invert_first()
            flip(0)
            back_second()
        else:
            take(tick - 1, (FWD1, FWD2))
            begin(tick, ACT_Q, q, act)
            advance_first()
            advance_second()
            take(tick - 1, (RET1, RET2, GRD1, GRD2))
            begin(tick, ACT_Y, y1, act)
            begin(tick, GRAD2, g2, same)
            invert_second()
            back_first()
        correlate(tick, 1, ACT_Y, g2[...])
        if last_tick:
            start_sums(1)
        if tick > 0:
            invert_first()
        correlate(tick, 0, ACT_IN, sent[tick, GRD1])
        if last_tick:
            start_sums(0)
        if tick > 0:
            back_second()
        if last_tick:
            pass_sums(1)
            pass_sums(0)

    finish_sums(1)
    finish_sums(0)
    take(ticks - 1, range(6))
    for index in range(2):
        for target in range(groups):
            pair_copy(index, target).wait_send()
        for step in range(1, groups):
            reduce_copy(index, step).wait_send()
    for tick in range(ticks):
        for field in range(6):
            pl.when(band > 0)(halo_copy(tick, field, 0).wait_send)
            pl.when(band < bands - 1)(halo_copy(tick, field, 1).wait_send)
            if field < RET1:
                pl.when(seg < segments - 1)(move_copy(tick, field).wait_send)
            else:
                pl.when(seg > 0)(move_copy(tick, field).wait_send)


def store(*refs):
    count = (len(refs) - 2) // 3
    sources, targets, held = refs[:count], refs[count:2 * count], refs[2 * count:3 * count]
    load_sem, store_sem = refs[3 * count:]
    loads = [pltpu.make_async_copy(sources[i], held[i], load_sem.at[i]) for i in range(count)]
    stores = [pltpu.make_async_copy(held[i], targets[i], store_sem.at[i]) for i in range(count)]
    for load in loads:
        load.start()
    for load, out in zip(loads, stores):
        load.wait()
        out.start()
    for out in stores:
        out.wait()


def local(forward_state, returning_state, returning_grad, weights, fresh_input, loss_grad):
    segments, bands = lax.axis_size("segment"), lax.axis_size("band")
    _, _, rows, width, channels = forward_state.shape
    pixels = rows * width
    ticks = fresh_input.shape[0]
    taps = weights.shape[2]
    chunk = taps // bands
    bf16, f32 = jnp.bfloat16, jnp.float32
    pair = jax.ShapeDtypeStruct((2, pixels, channels), bf16)
    dma = pltpu.SemaphoreType.DMA
    flat = lambda x: x.reshape(x.shape[:-3] + (pixels, channels))
    vmem = pl.BlockSpec(memory_space=pltpu.VMEM)
    outs = pl.pallas_call(
        functools.partial(kernel, ticks, segments, bands, width),
        out_shape=(pair, pair, pair, jax.ShapeDtypeStruct((2, chunk, channels), f32)),
        in_specs=[pl.BlockSpec(memory_space=pl.ANY)] * 6,
        out_specs=(vmem,) * 4,
        scratch_shapes=[
            pltpu.VMEM((2, pixels, channels), bf16),
            pltpu.VMEM((2, pixels, channels), bf16),
            pltpu.VMEM((2, pixels, channels), bf16),
            pltpu.VMEM((2, taps, channels), bf16),
            pltpu.VMEM((2, taps, channels), bf16),
            pltpu.VMEM((6, pixels + 2 * width, 3 * channels), bf16),
            pltpu.VMEM((ticks, 6, 2, width, channels), bf16),
            pltpu.VMEM((ticks, 6, 2, width, channels), bf16),
            pltpu.VMEM((ticks, 6, pixels, channels), bf16),
            pltpu.VMEM((max(ticks - 1, 1), 6, pixels, channels), bf16),
            pltpu.VMEM((2, taps, channels), f32),
            pltpu.VMEM((2, taps, channels), bf16),
            pltpu.VMEM((2, bands // 2, chunk, channels), bf16),
            pltpu.VMEM((2, bands // 2 - 1, chunk, channels), bf16),
            pltpu.VMEM((2, bands // 2 - 1, chunk, channels), bf16),
            dma((5,)),
            dma((ticks, 2)),
            dma((ticks, 6, 2)),
            dma((ticks, 6, 2)),
            dma((ticks, 6)),
            dma((ticks, 6)),
            dma((2, bands // 2)),
            dma((2, bands // 2)),
            dma((2, bands // 2 - 1)),
            dma((2, bands // 2 - 1)),
        ],
        compiler_params=pltpu.CompilerParams(
            collective_id=0, has_side_effects=True, vmem_limit_bytes=60 * 2**20),
    )(flat(forward_state[0]), flat(returning_state[0]), flat(returning_grad[0]), weights[0],
      flat(fresh_input), flat(loss_grad))
    outs = pl.pallas_call(
        store,
        out_shape=tuple(jax.ShapeDtypeStruct(o.shape, o.dtype) for o in outs),
        in_specs=[pl.BlockSpec(memory_space=pl.ANY)] * 4,
        out_specs=(pl.BlockSpec(memory_space=pl.ANY),) * 4,
        scratch_shapes=[pltpu.VMEM(o.shape, o.dtype) for o in outs] + [dma((4,)), dma((4,))],
    )(*outs)
    shape = forward_state.shape
    return tuple(o.reshape(shape) for o in outs[:3]) + (outs[3][None],)


def solution(mesh):
    pair = P("segment", None, "band", None, None)
    whole = P(None, None, "band", None, None)
    return jax.shard_map(
        local,
        mesh=mesh,
        in_specs=(pair, pair, pair, P("segment", None, None, None), whole, whole),
        out_specs=(pair, pair, pair, P("segment", None, "band", None)),
        check_vma=False,
    )
```
